256 devices in a mesh: mom: 4 (over y_hi, core), tr: 8 (over y_lo, x), tc: 8 (over z).
Axes of the slice: x: 4, y: 4 (y_hi: 2, y_lo: 2; y = y_hi * 2 + y_lo), z: 8, core: 2. Of those that a mesh axis runs over, the one named last changes fastest.
Arguments:
- start_rows: float32 [256, 8, 8192], P('tr', 'mom', 'tc'), may hold values from -6 to 6
- sigma_start: float32 [256, 8, 8192], P('tr', 'mom', 'tc'), may hold values from -6 to 6
- history: float32 [8, 8192, 8192], P('mom', 'tr', 'tc'), may hold values from -0.0625 to 0.0625
- interaction: float32 [2, 256, 8, 8192], P(None, 'tr', None, 'tc'), may hold values from -1.2 to 1.2
Outputs:
- first_rows: float32 [256, 8, 8192], P('tr', 'mom', 'tc')
- last_rows: float32 [256, 8, 8192], P('tr', 'mom', 'tc')
- last_sigma: float32 [256, 8, 8192], P('tr', 'mom', 'tc')
The draws below stay inside these ranges and needn't reach their ends.
All inputs are finite; a program needn't handle non-finite values.
Results may differ from the reference program's by a relative error of at most 0.00011.
Values sent between devices are 32-bit elements; how exact they have to be, the bound alone decides.
No kernel may reach another device: no remote copies, remote signals or barrier semaphores. Data moves between devices by JAX's collectives and lax.ppermute only.
A program may use at most 128 MiB of HBM per device.

```python
import jax
import jax.numpy as jnp
from jax import lax

NT = 8192
ROWS = 256
BLOCKS = 2
CORRECTORS = 2
KMOM = 8


def shard_levels(own_key, dims, shards, least, high):
    def one(position, parts):
        steps = jax.random.uniform(jax.random.fold_in(jax.random.fold_in(own_key, 6), position), (parts,), jnp.float32, least / len(shards), high / len(shards))
        return jnp.repeat(jnp.exp(steps), dims[position] // parts).reshape((-1,) + (1,) * (len(dims) - position - 1))

    loudness = one(*shards[0])
    for cut in shards[1:]:
        loudness = loudness * one(*cut)
    return loudness


def centred(stream_key, shape, width, limit, split=(), dtype=jnp.bfloat16):
    entries = width * jax.random.normal(stream_key, shape, jnp.float32)
    if split:
        entries = entries * shard_levels(stream_key, shape, split, -0.22, 0.18)
    return jnp.clip(entries, -limit, limit).astype(dtype)


def setup_inputs(seed: int = 0) -> dict:
    key_of = jax.random.split(jax.random.key(seed), 5)
    start_rows = centred(key_of[0], (ROWS, KMOM, NT), 1.0, 6.0, ((0, 8), (1, 4), (2, 8)), jnp.float32)
    sigma_start = centred(key_of[1], (ROWS, KMOM, NT), 1.0, 6.0, ((0, 8), (1, 4), (2, 8)), jnp.float32)
    history = centred(key_of[2], (KMOM, NT, NT), NT ** -0.5, 0.0625, ((0, 4), (1, 8), (2, 8)), jnp.float32)
    interaction = centred(key_of[3], (BLOCKS, ROWS, KMOM, NT), 0.2, 1.2, ((1, 8), (3, 8)), jnp.float32)
    return dict(start_rows=start_rows, sigma_start=sigma_start, history=history, interaction=interaction)


def convolve(weights_now, green):
    result = jnp.zeros(green.shape, jnp.float32)
    for shift_index in range(KMOM):
        result = result + weights_now[:, shift_index:shift_index + 1, :] * jnp.roll(green, shift_index, axis=1)
    return result


def reference(start_rows, sigma_start, history, interaction):
    green = start_rows
    energy = sigma_start
    results = []
    for block_index in range(BLOCKS):
        base_rows = green
        for sweep_index in range(CORRECTORS):
            green = base_rows + jnp.einsum('rkt,ktc->rkc', energy, history, precision=lax.Precision.HIGHEST)
            energy = convolve(interaction[block_index], green)
        results.append(green)
    return results[0], results[BLOCKS - 1], energy
```

```python
import jax
import jax.numpy as jnp
from jax import lax
from jax.sharding import PartitionSpec as P

CORRECTORS = 2
GROUPS = 1
ALL = ("mom", "tr", "tc")


def ring(size, step):
    return [(k, (k + step) % size) for k in range(size)]


def along_x(step):
    return [(y * 4 + x, y * 4 + (x + step) % 4) for y in range(2) for x in range(4)]


Y_PAIR = [(y * 4 + x, (1 - y) * 4 + x) for y in range(2) for x in range(4)]


def turn(flip):
    return [
        ((m * 8 + i) * 8 + j, ((m ^ flip) * 8 + j) * 8 + i)
        for i in range(8)
        for m in range(4)
        for j in range(8)
    ]


def pick(pieces, index):
    stacked = jnp.stack(pieces)
    return lax.dynamic_index_in_dim(stacked, index, 0, keepdims=False)


def by_xor(pieces, me):
    low = (me & 1) == 1
    high = (me & 2) == 2
    a, b, c, d = pieces
    a, b, c, d = (
        jnp.where(low, b, a),
        jnp.where(low, a, b),
        jnp.where(low, d, c),
        jnp.where(low, c, d),
    )
    return (
        jnp.where(high, c, a),
        jnp.where(high, d, b),
        jnp.where(high, a, c),
        jnp.where(high, b, d),
    )


def gather_tc(piece):
    up = down = piece
    ups, downs = [], []
    for _ in range(3):
        up = lax.ppermute(up, "tc", ring(8, 1))
        down = lax.ppermute(down, "tc", ring(8, -1))
        ups.append(up)
        downs.append(down)
    half = piece.shape[1] // 2
    far = jnp.concatenate(
        [
            lax.ppermute(up[:, :half], "tc", ring(8, 1)),
            lax.ppermute(down[:, half:], "tc", ring(8, -1)),
        ],
        axis=1,
    )
    return [piece, *downs, far, *ups[::-1]]


def sum_tr(partial, start, x, y, z):
    count, total, width = partial.shape
    blocks = partial.reshape(count, 8, total // 8, width)

    def block(yy, xx):
        return lax.dynamic_index_in_dim(blocks, (yy * 4 + xx % 4 - z) % 8, 1, keepdims=False)

    from_low = lax.ppermute(block(0, x + 2), "tr", along_x(1))
    from_high = lax.ppermute(block(1, x + 2), "tr", along_x(-1))
    to_high = jnp.stack([block(0, x + 1) + from_low, block(1, x + 1)])
    to_low = jnp.stack([block(0, x + 3), block(1, x + 3) + from_high])
    got_low = lax.ppermute(to_high, "tr", along_x(1))
    got_high = lax.ppermute(to_low, "tr", along_x(-1))
    sums = [block(half, x) + got_low[half] + got_high[half] for half in range(2)]
    other = jnp.where(y == 0, sums[1], sums[0])
    mine = jnp.where(y == 0, sums[0], sums[1])
    return start + mine + lax.ppermute(other, "tr", Y_PAIR)


def quarters(value):
    return jnp.split(value, 4, axis=2)


def convolve(weights, green, me):
    parts = by_xor(quarters(green), me)
    arrived = [parts[0]]
    for flip in range(1, 4):
        arrived.append(lax.ppermute(parts[flip], "mom", [(m, m ^ flip) for m in range(4)]))
    pairs = by_xor(arrived, me)
    rows = [pairs[k // 2][k % 2] for k in range(8)]
    energy = []
    for k in range(8):
        energy.append(sum(weights[d] * rows[(k - d) % 8] for d in range(8)))
    return by_xor([jnp.stack(energy[2 * p : 2 * p + 2]) for p in range(4)], me)


def body(start_rows, sigma_start, history, interaction):
    me = lax.axis_index("mom")
    place = lax.axis_index("tr")
    z = lax.axis_index("tc")
    x, y = place % 4, place // 4
    width = start_rows.shape[2] // 4
    weights = lax.dynamic_slice_in_dim(interaction, me * width, width, 3).transpose(0, 2, 1, 3)

    def split(value):
        return jnp.split(value, GROUPS, axis=1)

    green = split(start_rows.transpose(1, 0, 2))
    blocks = interaction.shape[0]
    weights = [split(weights[b]) for b in range(blocks)]
    spread = [lax.ppermute(e, ALL, turn(0)) for e in split(sigma_start.transpose(1, 0, 2))]
    results = []
    for b in range(blocks):
        base = green
        for sweep in range(CORRECTORS):
            last = b == blocks - 1 and sweep == CORRECTORS - 1
            green, following = [], []
            for g in range(GROUPS):
                gathered = jnp.concatenate(gather_tc(spread[g]), axis=1)
                partial = jnp.einsum(
                    "mrt,mtc->mrc",
                    gathered,
                    history,
                    precision=lax.Precision.HIGH,
                    preferred_element_type=jnp.float32,
                )
                rows = sum_tr(partial, base[g], x, y, z)
                green.append(rows)
                parts = convolve(weights[b][g], rows, me)
                if last:
                    back = [parts[0]] + [
                        lax.ppermute(parts[f], "mom", [(m, m ^ f) for m in range(4)])
                        for f in range(1, 4)
                    ]
                else:
                    back = [lax.ppermute(parts[f], ALL, turn(f)) for f in range(4)]
                following.append(jnp.concatenate(by_xor(back, me), axis=2))
            spread = following
        results.append(green)

    def whole(groups):
        return jnp.concatenate(groups, axis=1).transpose(1, 0, 2)

    return whole(results[0]), whole(results[-1]), whole(spread)


def solution(mesh):
    return jax.shard_map(
        body,
        mesh=mesh,
        in_specs=(
            P("tr", "mom", "tc"),
            P("tr", "mom", "tc"),
            P("mom", "tr", "tc"),
            P(None, "tr", None, "tc"),
        ),
        out_specs=(P("tr", "mom", "tc"), P("tr", "mom", "tc"), P("tr", "mom", "tc")),
        check_vma=False,
    )
```

```python
import jax
import jax.numpy as jnp
from jax import lax
from jax.sharding import PartitionSpec as P

CORRECTORS = 2
ALL = ("mom", "tr", "tc")
PLANE = ("mom", "tr")


def ring(step):
    return [(k, (k + step) % 8) for k in range(8)]


def along_x(step):
    return [(y * 4 + x, y * 4 + (x + step) % 4) for y in range(2) for x in range(4)]


def plane_flip(high, low, core):
    flip = 2 * high + core
    return [(m * 8 + i, (m ^ flip) * 8 + (i ^ (4 * low))) for m in range(4) for i in range(8)]


def turn(high):
    return [
        ((m * 8 + i) * 8 + j, ((m ^ (2 * high)) * 8 + j) * 8 + i)
        for m in range(4)
        for i in range(8)
        for j in range(8)
    ]


def swap(bit, first, second):
    return jnp.where(bit == 0, first, second), jnp.where(bit == 0, second, first)


def halves(value):
    return jnp.split(value, 2, axis=-1)


def gather_tc(chain, odd):
    up = down = chain
    ups, downs = [], []
    for _ in range(3):
        up = lax.ppermute(up, "tc", ring(1))
        down = lax.ppermute(down, "tc", ring(-1))
        ups.append(up)
        downs.append(down)
    far = lax.ppermute(down, "tc", ring(-1)) if odd else lax.ppermute(up, "tc", ring(1))
    return jnp.concatenate([chain, *downs, far, *ups[::-1]])


def sum_x(partial, x, z):
    blocks = partial.reshape(8, partial.shape[0] // 8, partial.shape[1])

    def block(yy, xx):
        return lax.dynamic_index_in_dim(blocks, (yy * 4 + xx % 4 - z) % 8, 0, keepdims=False)

    from_low = lax.ppermute(block(0, x + 2), "tr", along_x(1))
    from_high = lax.ppermute(block(1, x + 2), "tr", along_x(-1))
    to_high = jnp.stack([block(0, x + 1) + from_low, block(1, x + 1)])
    to_low = jnp.stack([block(0, x + 3), block(1, x + 3) + from_high])
    got_low = lax.ppermute(to_high, "tr", along_x(1))
    got_high = lax.ppermute(to_low, "tr", along_x(-1))
    return jnp.stack([block(0, x), block(1, x)]) + got_low + got_high


def sum_y(sums, low, high):
    near, far = swap(high, *halves(sums))
    near_own, near_other = swap(low, near[0], near[1])
    far_own, far_other = swap(low, far[0], far[1])
    a = lax.ppermute(far_own, PLANE, plane_flip(1, 0, 0))
    b = lax.ppermute(far_other, PLANE, plane_flip(1, 1, 0))
    c = lax.ppermute(near_other, PLANE, plane_flip(0, 1, 0))
    return jnp.stack(swap(high, near_own + c, a + b))


def convolve(weights, green, core):
    other = lax.ppermute(green, PLANE, plane_flip(0, 0, 1))
    second, fourth = swap(core, other[0], other[1])
    rows = [*green[0], *second, *green[1], *fourth]
    energy = [sum(weights[d] * rows[(k - d) % 8] for d in range(8)) for k in (0, 1, 4, 5)]
    return jnp.stack([jnp.stack(energy[:2]), jnp.stack(energy[2:])])


def turned(energy, high):
    stay, cross = swap(high, energy[0], energy[1])
    got = [lax.ppermute(stay, ALL, turn(0)), lax.ppermute(cross, ALL, turn(1))]
    return jnp.concatenate(swap(high, *got), axis=-1)


def to_half(value, high):
    mine, other = swap(high, *halves(value))
    return jnp.stack(swap(high, mine, lax.ppermute(other, PLANE, plane_flip(1, 0, 0))))


def from_half(value, high):
    mine, other = swap(high, value[0], value[1])
    got = lax.ppermute(other, PLANE, plane_flip(1, 0, 0))
    return jnp.concatenate(swap(high, mine, got), axis=-1)


def body(start_rows, sigma_start, history, interaction):
    me = lax.axis_index("mom")
    place = lax.axis_index("tr")
    z = lax.axis_index("tc")
    x, low = place % 4, place // 4
    high, core = me // 2, me % 2
    width = start_rows.shape[2] // 2
    spread = lax.ppermute(sigma_start.transpose(1, 0, 2), ALL, turn(0))
    weights = lax.dynamic_slice_in_dim(interaction, high * width, width, 3)
    weights = weights.transpose(0, 2, 1, 3)
    green = to_half(start_rows.transpose(1, 0, 2), high)
    blocks = interaction.shape[0]
    results = []
    for b in range(blocks):
        base = green
        for sweep in range(CORRECTORS):
            sums = []
            for k in range(2):
                partial = jnp.dot(
                    gather_tc(spread[k], k),
                    history[k],
                    precision=lax.Precision.HIGH,
                    preferred_element_type=jnp.float32,
                )
                sums.append(sum_x(partial, x, z))
            green = base + sum_y(jnp.stack(sums, axis=1), low, high)
            energy = convolve(weights[b], green, core)
            if not (b == blocks - 1 and sweep == CORRECTORS - 1):
                spread = turned(energy, high)
        results.append(green)
    first = from_half(results[0], high)
    last, sigma = from_half(jnp.stack([results[-1], energy], axis=1), high)
    return tuple(v.transpose(1, 0, 2) for v in (first, last, sigma))


def solution(mesh):
    return jax.shard_map(
        body,
        mesh=mesh,
        in_specs=(
            P("tr", "mom", "tc"),
            P("tr", "mom", "tc"),
            P("mom", "tr", "tc"),
            P(None, "tr", None, "tc"),
        ),
        out_specs=(P("tr", "mom", "tc"), P("tr", "mom", "tc"), P("tr", "mom", "tc")),
        check_vma=False,
    )
```

```python
import jax
import jax.numpy as jnp
from jax import lax
from jax.sharding import PartitionSpec as P

CORRECTORS = 2
ALL = ("mom", "tr", "tc")
PLANE = ("mom", "tr")


def ring(step):
    return [(k, (k + step) % 8) for k in range(8)]


def along_x(step):
    return [(y * 4 + x, y * 4 + (x + step) % 4) for y in range(2) for x in range(4)]


def plane_flip(high, low, core):
    flip = 2 * high + core
    return [(m * 8 + i, (m ^ flip) * 8 + (i ^ (4 * low))) for m in range(4) for i in range(8)]


def mirror(high, offset):
    return [
        ((m * 8 + i) * 8 + j, ((m ^ (2 * high)) * 8 + i) * 8 + (i - j + offset) % 8)
        for m in range(4)
        for i in range(8)
        for j in range(8)
    ]


def slide(offset):
    return [(i * 8 + b, (i - b + offset) % 8 * 8 + b) for i in range(8) for b in range(8)]


def swap(bit, first, second):
    return jnp.where(bit == 0, first, second), jnp.where(bit == 0, second, first)


def halves(value):
    return jnp.split(value, 2, axis=-1)


def gather_tc(chain, odd):
    up = down = chain
    ups, downs = [], []
    for _ in range(3):
        up = lax.ppermute(up, "tc", ring(1))
        down = lax.ppermute(down, "tc", ring(-1))
        ups.append(up)
        downs.append(down)
    far = lax.ppermute(down, "tc", ring(-1)) if odd else lax.ppermute(up, "tc", ring(1))
    return jnp.concatenate([chain, *downs, far, *ups[::-1]])


def sum_x(partial, x, z):
    blocks = partial.reshape(8, partial.shape[0] // 8, partial.shape[1])

    def block(yy, xx):
        return lax.dynamic_index_in_dim(blocks, (yy * 4 + xx % 4 - z) % 8, 0, keepdims=False)

    from_low = lax.ppermute(block(0, x + 2), "tr", along_x(1))
    from_high = lax.ppermute(block(1, x + 2), "tr", along_x(-1))
    to_high = jnp.stack([block(0, x + 1) + from_low, block(1, x + 1)])
    to_low = jnp.stack([block(0, x + 3), block(1, x + 3) + from_high])
    got_low = lax.ppermute(to_high, "tr", along_x(1))
    got_high = lax.ppermute(to_low, "tr", along_x(-1))
    return jnp.stack([block(0, x), block(1, x)]) + got_low + got_high


def sum_y(sums, low, high):
    near, far = swap(high, *halves(sums))
    near_own, near_other = swap(low, near[0], near[1])
    far_own, far_other = swap(low, far[0], far[1])
    a = lax.ppermute(far_own, PLANE, plane_flip(1, 0, 0))
    b = lax.ppermute(far_other, PLANE, plane_flip(1, 1, 0))
    c = lax.ppermute(near_other, PLANE, plane_flip(0, 1, 0))
    return jnp.stack(swap(high, near_own + c, a + b))


def convolve(weights, green, core):
    other = lax.ppermute(green, PLANE, plane_flip(0, 0, 1))
    second, fourth = swap(core, other[0], other[1])
    rows = [*green[0], *second, *green[1], *fourth]
    energy = [sum(weights[d] * rows[(k - d) % 8] for d in range(8)) for k in (0, 1, 4, 5)]
    return jnp.stack([jnp.stack(energy[:2]), jnp.stack(energy[2:])])


def turned(energy, high):
    result = []
    for k in range(2):
        stay, cross = swap(high, energy[0, k], energy[1, k])
        got = [lax.ppermute(stay, ALL, mirror(0, k)), lax.ppermute(cross, ALL, mirror(1, k))]
        whole = jnp.concatenate(swap(high, *got), axis=-1)
        result.append(lax.ppermute(whole, ("tr", "tc"), slide(k)))
    return result


def to_half(value, high):
    mine, other = swap(high, *halves(value))
    return jnp.stack(swap(high, mine, lax.ppermute(other, PLANE, plane_flip(1, 0, 0))))


def from_half(value, high):
    mine, other = swap(high, value[0], value[1])
    got = lax.ppermute(other, PLANE, plane_flip(1, 0, 0))
    return jnp.concatenate(swap(high, mine, got), axis=-1)


def body(start_rows, sigma_start, history, interaction):
    me = lax.axis_index("mom")
    place = lax.axis_index("tr")
    z = lax.axis_index("tc")
    x, low = place % 4, place // 4
    high, core = me // 2, me % 2
    width = start_rows.shape[2] // 2
    spread = []
    for k in range(2):
        half_way = lax.ppermute(sigma_start[:, k], ALL, mirror(0, k))
        spread.append(lax.ppermute(half_way, ("tr", "tc"), slide(k)))
    weights = lax.dynamic_slice_in_dim(interaction, high * width, width, 3)
    weights = weights.transpose(0, 2, 1, 3)
    green = to_half(start_rows.transpose(1, 0, 2), high)
    blocks = interaction.shape[0]
    results = []
    for b in range(blocks):
        base = green
        for sweep in range(CORRECTORS):
            sums = []
            for k in range(2):
                partial = jnp.dot(
                    gather_tc(spread[k], k),
                    history[k],
                    precision=lax.Precision.HIGH,
                    preferred_element_type=jnp.float32,
                )
                sums.append(sum_x(partial, x, z + place - k))
            green = base + sum_y(jnp.stack(sums, axis=1), low, high)
            energy = convolve(weights[b], green, core)
            if not (b == blocks - 1 and sweep == CORRECTORS - 1):
                spread = turned(energy, high)
        results.append(green)
    first = from_half(results[0], high)
    last, sigma = from_half(jnp.stack([results[-1], energy], axis=1), high)
    return tuple(v.transpose(1, 0, 2) for v in (first, last, sigma))


def solution(mesh):
    return jax.shard_map(
        body,
        mesh=mesh,
        in_specs=(
            P("tr", "mom", "tc"),
            P("tr", "mom", "tc"),
            P("mom", "tr", "tc"),
            P(None, "tr", None, "tc"),
        ),
        out_specs=(P("tr", "mom", "tc"), P("tr", "mom", "tc"), P("tr", "mom", "tc")),
        check_vma=False,
    )
```

```python
import jax
import jax.numpy as jnp
from jax import lax
from jax.sharding import PartitionSpec as P

CORRECTORS = 2
ALL = ("mom", "tr", "tc")
PLANE = ("mom", "tr")


def ring(step):
    return [(k, (k + step) % 8) for k in range(8)]


def along_x(step):
    return [(y * 4 + x, y * 4 + (x + step) % 4) for y in range(2) for x in range(4)]


def plane_flip(high, low, core):
    flip = 2 * high + core
    return [(m * 8 + i, (m ^ flip) * 8 + (i ^ (4 * low))) for m in range(4) for i in range(8)]


def mirror(high, offset):
    return [
        ((m * 8 + i) * 8 + j, ((m ^ (2 * high)) * 8 + i) * 8 + (i - j + offset) % 8)
        for m in range(4)
        for i in range(8)
        for j in range(8)
    ]


def slide(offset):
    return [(i * 8 + b, (i - b + offset) % 8 * 8 + b) for i in range(8) for b in range(8)]


def swap(bit, first, second):
    return jnp.where(bit == 0, first, second), jnp.where(bit == 0, second, first)


def halves(value):
    return jnp.split(value, 2, axis=-1)


def gather_tc(chain, odd):
    up = down = chain
    ups, downs = [], []
    for _ in range(3):
        up = lax.ppermute(up, "tc", ring(1))
        down = lax.ppermute(down, "tc", ring(-1))
        ups.append(up)
        downs.append(down)
    far = lax.ppermute(down, "tc", ring(-1)) if odd else lax.ppermute(up, "tc", ring(1))
    return jnp.concatenate([chain, *downs, far, *ups[::-1]])


def sum_x(partial, x, z):
    blocks = partial.reshape(8, partial.shape[0] // 8, partial.shape[1])

    def block(yy, xx):
        return lax.dynamic_index_in_dim(blocks, (yy * 4 + xx % 4 - z) % 8, 0, keepdims=False)

    from_low = lax.ppermute(block(0, x + 2), "tr", along_x(1))
    from_high = lax.ppermute(block(1, x + 2), "tr", along_x(-1))
    to_high = jnp.stack([block(0, x + 1) + from_low, block(1, x + 1)])
    to_low = jnp.stack([block(0, x + 3), block(1, x + 3) + from_high])
    got_low = lax.ppermute(to_high, "tr", along_x(1))
    got_high = lax.ppermute(to_low, "tr", along_x(-1))
    return jnp.stack([block(0, x), block(1, x)]) + got_low + got_high


def sum_y(sums, low, high):
    near, far = swap(high, *halves(sums))
    near_own, near_other = swap(low, near[0], near[1])
    far_own, far_other = swap(low, far[0], far[1])
    a = lax.ppermute(far_own, PLANE, plane_flip(1, 0, 0))
    b = lax.ppermute(far_other, PLANE, plane_flip(1, 1, 0))
    c = lax.ppermute(near_other, PLANE, plane_flip(0, 1, 0))
    return jnp.stack(swap(high, near_own + c, a + b))


def convolve(weights, green, core):
    other = lax.ppermute(green, PLANE, plane_flip(0, 0, 1))
    second, fourth = swap(core, other[0], other[1])
    rows = [*green[0], *second, *green[1], *fourth]
    energy = [sum(weights[d] * rows[(k - d) % 8] for d in range(8)) for k in (0, 1, 4, 5)]
    return jnp.stack([jnp.stack(energy[:2]), jnp.stack(energy[2:])])


def turned(energy, high):
    result = []
    for k in range(2):
        stay, cross = swap(high, energy[0, k], energy[1, k])
        got = [lax.ppermute(stay, ALL, mirror(0, k)), lax.ppermute(cross, ALL, mirror(1, k))]
        whole = jnp.concatenate(swap(high, *got), axis=-1)
        result.append(lax.ppermute(whole, ("tr", "tc"), slide(k)))
    return result


def to_half(value, high):
    mine, other = swap(high, *halves(value))
    return jnp.stack(swap(high, mine, lax.ppermute(other, PLANE, plane_flip(1, 0, 0))))


def from_half(value, high):
    mine, other = swap(high, value[0], value[1])
    got = lax.ppermute(other, PLANE, plane_flip(1, 0, 0))
    return jnp.concatenate(swap(high, mine, got), axis=-1)


def body(start_rows, sigma_start, history, interaction):
    me = lax.axis_index("mom")
    place = lax.axis_index("tr")
    z = lax.axis_index("tc")
    x, low = place % 4, place // 4
    high, core = me // 2, me % 2
    width = start_rows.shape[2] // 2
    spread = []
    for k in range(2):
        half_way = lax.ppermute(sigma_start[:, k], ALL, mirror(0, k))
        spread.append(lax.ppermute(half_way, ("tr", "tc"), slide(k)))
    weights = lax.dynamic_slice_in_dim(interaction, high * width, width, 3)
    weights = weights.transpose(0, 2, 1, 3)
    green = to_half(start_rows.transpose(1, 0, 2), high)
    blocks = interaction.shape[0]
    results = []
    for b in range(blocks):
        base = green
        for sweep in range(CORRECTORS):
            sums = []
            for k in range(2):
                partial = jnp.dot(
                    gather_tc(spread[k], k),
                    history[k],
                    precision=lax.Precision.HIGH,
                    preferred_element_type=jnp.float32,
                )
                sums.append(sum_y(sum_x(partial, x, z + place - k), low, high))
            green = base + jnp.stack(sums, axis=1)
            energy = convolve(weights[b], green, core)
            if not (b == blocks - 1 and sweep == CORRECTORS - 1):
                spread = turned(energy, high)
        results.append(green)
    first = from_half(results[0], high)
    last, sigma = from_half(jnp.stack([results[-1], energy], axis=1), high)
    return tuple(v.transpose(1, 0, 2) for v in (first, last, sigma))


def solution(mesh):
    return jax.shard_map(
        body,
        mesh=mesh,
        in_specs=(
            P("tr", "mom", "tc"),
            P("tr", "mom", "tc"),
            P("mom", "tr", "tc"),
            P(None, "tr", None, "tc"),
        ),
        out_specs=(P("tr", "mom", "tc"), P("tr", "mom", "tc"), P("tr", "mom", "tc")),
        check_vma=False,
    )
```

```python
import jax
import jax.numpy as jnp
from jax import lax
from jax.sharding import PartitionSpec as P

CORRECTORS = 2
ALL = ("mom", "tr", "tc")
PLANE = ("mom", "tr")


def ring(step):
    return [(k, (k + step) % 8) for k in range(8)]


def along_x(step):
    return [(y * 4 + x, y * 4 + (x + step) % 4) for y in range(2) for x in range(4)]


def plane_flip(high, low, core):
    flip = 2 * high + core
    return [(m * 8 + i, (m ^ flip) * 8 + (i ^ (4 * low))) for m in range(4) for i in range(8)]


def mirror(high, offset):
    return [
        ((m * 8 + i) * 8 + j, ((m ^ (2 * high)) * 8 + i) * 8 + (i - j + offset) % 8)
        for m in range(4)
        for i in range(8)
        for j in range(8)
    ]


def slide(offset):
    return [(i * 8 + b, (i - b + offset) % 8 * 8 + b) for i in range(8) for b in range(8)]


def swap(bit, first, second):
    return jnp.where(bit == 0, first, second), jnp.where(bit == 0, second, first)


def halves(value):
    return jnp.split(value, 2, axis=-1)


def gather_tc(chain, odd):
    up = down = chain
    ups, downs = [], []
    for _ in range(3):
        up = lax.ppermute(up, "tc", ring(1))
        down = lax.ppermute(down, "tc", ring(-1))
        ups.append(up)
        downs.append(down)
    far = lax.ppermute(down, "tc", ring(-1)) if odd else lax.ppermute(up, "tc", ring(1))
    return jnp.concatenate([chain, *downs, far, *ups[::-1]])


def sum_x(partial, x, z):
    blocks = partial.reshape(8, partial.shape[0] // 8, partial.shape[1])

    def block(yy, xx):
        return lax.dynamic_index_in_dim(blocks, (yy * 4 + xx % 4 - z) % 8, 0, keepdims=False)

    from_low = lax.ppermute(block(0, x + 2), "tr", along_x(1))
    from_high = lax.ppermute(block(1, x + 2), "tr", along_x(-1))
    to_high = jnp.stack([block(0, x + 1) + from_low, block(1, x + 1)])
    to_low = jnp.stack([block(0, x + 3), block(1, x + 3) + from_high])
    got_low = lax.ppermute(to_high, "tr", along_x(1))
    got_high = lax.ppermute(to_low, "tr", along_x(-1))
    return jnp.stack([block(0, x), block(1, x)]) + got_low + got_high


def sum_y(sums, low, high):
    near, far = swap(high, *halves(sums))
    near_own, near_other = swap(low, near[0], near[1])
    far_own, far_other = swap(low, far[0], far[1])
    a = lax.ppermute(far_own, PLANE, plane_flip(1, 0, 0))
    b = lax.ppermute(far_other, PLANE, plane_flip(1, 1, 0))
    c = lax.ppermute(near_other, PLANE, plane_flip(0, 1, 0))
    return jnp.stack(swap(high, near_own + c, a + b))


def convolve(weights, green, core):
    other = lax.ppermute(green, PLANE, plane_flip(0, 0, 1))
    second, fourth = swap(core, other[0], other[1])
    rows = [*green[0], *second, *green[1], *fourth]
    energy = [sum(weights[d] * rows[(k - d) % 8] for d in range(8)) for k in (0, 1, 4, 5)]
    return jnp.stack([jnp.stack(energy[:2]), jnp.stack(energy[2:])])


def turned(energy, high):
    result = []
    for k in range(2):
        stay, cross = swap(high, energy[0, k], energy[1, k])
        got = [lax.ppermute(stay, ALL, mirror(0, k)), lax.ppermute(cross, ALL, mirror(1, k))]
        whole = jnp.concatenate(swap(high, *got), axis=-1)
        result.append(lax.ppermute(whole, ("tr", "tc"), slide(k)))
    return result


def to_half(value, high):
    mine, other = swap(high, *halves(value))
    return jnp.stack(swap(high, mine, lax.ppermute(other, PLANE, plane_flip(1, 0, 0))))


def from_half(value, high):
    mine, other = swap(high, value[0], value[1])
    got = lax.ppermute(other, PLANE, plane_flip(1, 0, 0))
    return jnp.concatenate(swap(high, mine, got), axis=-1)


def body(start_rows, sigma_start, history, interaction):
    me = lax.axis_index("mom")
    place = lax.axis_index("tr")
    z = lax.axis_index("tc")
    x, low = place % 4, place // 4
    high, core = me // 2, me % 2
    width = start_rows.shape[2] // 2
    spread = []
    for k in range(2):
        half_way = lax.ppermute(sigma_start[:, k], ALL, mirror(0, k))
        spread.append(lax.ppermute(half_way, ("tr", "tc"), slide(k)))
    weights = lax.dynamic_slice_in_dim(interaction, high * width, width, 3)
    weights = weights.transpose(0, 2, 1, 3)
    green = to_half(start_rows.transpose(1, 0, 2), high)
    blocks = interaction.shape[0]
    results = []
    for b in range(blocks):
        base = green
        for sweep in range(CORRECTORS):
            sums = []
            for k in range(2):
                partial = jnp.dot(
                    gather_tc(spread[k], k),
                    history[k],
                    precision=lax.Precision.HIGH,
                    preferred_element_type=jnp.float32,
                )
                sums.append(sum_y(sum_x(partial, x, z + place - k), low, high))
            green = base + jnp.stack(sums, axis=1)
            energy = convolve(weights[b], green, core)
            if not (b == blocks - 1 and sweep == CORRECTORS - 1):
                spread = turned(energy, high)
        results.append(green)
    first = from_half(results[0], high)
    last, sigma = from_half(results[-1], high), from_half(energy, high)
    return tuple(v.transpose(1, 0, 2) for v in (first, last, sigma))


def solution(mesh):
    return jax.shard_map(
        body,
        mesh=mesh,
        in_specs=(
            P("tr", "mom", "tc"),
            P("tr", "mom", "tc"),
            P("mom", "tr", "tc"),
            P(None, "tr", None, "tc"),
        ),
        out_specs=(P("tr", "mom", "tc"), P("tr", "mom", "tc"), P("tr", "mom", "tc")),
        check_vma=False,
    )
```
